32 devices in a mesh: groups: 2 (over y), expert: 4 (over z), tensor: 2 (over x), inner: 2 (over core).
Axes of the slice: x: 2, y: 2, z: 4, core: 2. Of those that a mesh axis runs over, the one named last changes fastest.
Arguments:
- tokens: bfloat16 [1024, 7168], P(('groups', 'expert'), ('tensor', 'inner')), parts along dimension 0, may hold values from -6 to 6
- expert_ids: int32 [1024, 8], P(('groups', 'expert')), parts along dimension 0, may hold values from 0 to 31, all different within a row; in each aligned block of 128 rows (0 to 127, 128 to 255, ...) at most 96 rows name the same one
- gate_weights: float32 [1024, 8], P(('groups', 'expert')), parts along dimension 0, may hold values from 0.05 to 0.45
- base_weights: bfloat16 [3, 1024, 7168], P(None, 'expert', ('tensor', 'inner')), may hold values from -0.0625 to 0.0625
- in_factor: bfloat16 [3840, 7168], P('expert', ('tensor', 'inner')), may hold values from -0.0625 to 0.0625
- out_factors: bfloat16 [2, 3840, 1024], P(None, 'expert', ('tensor', 'inner')), may hold values from -0.375 to 0.375
- ranks: int32 [32], P('expert'), may hold values from 64 to 512, as said below
Outputs:
- mixed: bfloat16 [1024, 7168], P(('groups', 'expert'), ('tensor', 'inner')), parts along dimension 0
The draws below stay inside these ranges and needn't reach their ends.
There are 2 independent parts, one for each index of `groups`. The reference program is written for one: setup_inputs(seed, part) draws one part's arguments, and reference() takes and returns one part's arrays. A program takes and returns all parts, laid end to end along the dimension named above; an argument that names none is the same for every part. Nothing has to cross between parts.
Inputs may be any that keep to these rules, and one draw needn't show every extreme that they name: `expert_ids`: in each aligned block of 128 tokens no expert is chosen more than 96 times, and some expert is chosen exactly 96 times; the experts of one token differ. The ranks of each aligned block of 8 experts sum to exactly 960.
All inputs are finite; a program needn't handle non-finite values.
Results may differ from the reference program's by a relative error of at most 0.023.
Values may be sent and summed in bfloat16 or wider, within the bound.
No kernel may reach another device: no remote copies, remote signals or barrier semaphores. Data moves between devices by JAX's collectives and lax.ppermute only.
A program may use at most 64 MiB of HBM per device.

```python
import math
import jax
import jax.numpy as jnp
import numpy as np
from jax import lax

D = 7168
F = 1024
TOP = 8
EXP_DEV = 8
TOK_E = 128
RANK_MIN = 64
RANK_MAX = 512
EXPERTS = 32
TOKENS = 512
CAP = 96
RANKS_ALL = 3840
N_EXPERT = 4
N_TENSOR = 2
N_INNER = 2


def draw_ranks(key, part):
    groups_count = EXPERTS // EXP_DEV
    extra = RANK_MAX - RANK_MIN
    first, second, third = jax.random.split(key, 3)
    cuts = jnp.sort(jax.random.randint(first, (groups_count, EXP_DEV - 1), 0, extra + 1), axis=1)
    edges = jnp.concatenate([jnp.zeros((groups_count, 1), jnp.int32), cuts.astype(jnp.int32), jnp.full((groups_count, 1), extra, jnp.int32)], 1)
    shares = edges[:, 1:] - edges[:, :-1]
    chosen = jax.random.randint(second, (), 0, groups_count)
    single = jax.random.randint(third, (), 0, EXP_DEV)
    forced = jnp.where(jnp.arange(EXP_DEV) == single, extra, 0).astype(jnp.int32)
    shares = jnp.where((jnp.arange(groups_count) == chosen)[:, None], forced[None, :], shares)
    return (RANK_MIN + shares).reshape(EXPERTS).astype(jnp.int32)


def level_of(own_key, shape, cuts, least, top_value):
    loudness = 1.0
    for axis_at, blocks in cuts:
        draws = jax.random.uniform(jax.random.fold_in(jax.random.fold_in(own_key, 6), axis_at), (blocks,), jnp.float32, least / len(cuts), top_value / len(cuts))
        loudness = loudness * jnp.repeat(jnp.exp(draws), shape[axis_at] // blocks).reshape((-1,) + (1,) * (len(shape) - 1 - axis_at))
    return loudness


def deal_out(key, own, number, rows, count, top, bound, slope):
    ranking = jax.random.permutation(key, count)
    packed, usual = load_shares(count, rows * top, bound, slope, True), load_shares(count, rows * top, bound, slope, False)
    places = jnp.arange(count)

    def named(sizes, turn):
        used = int((sizes > 0).sum())
        fixed = max(1, used // 4)
        passed = fixed + (places - fixed + turn * (used - fixed)) % max(1, count - fixed)
        return jnp.zeros((count,), jnp.int32).at[ranking[jnp.where(places < fixed, places, passed)]].set(jnp.asarray(sizes, jnp.int32))

    sizes = jnp.where(number % 4 == 0, named(packed, number // 4), named(usual, number - number // 4 - 1))
    mixed = jax.random.permutation(jax.random.fold_in(own, 3), count)
    donor, receiver = mixed[0:count // 2 * 2:2], mixed[1:count // 2 * 2:2]
    slack = jnp.minimum(sizes[donor] - 1, bound - sizes[receiver]) // 2
    slack = jnp.where((donor == ranking[0]) | (receiver == ranking[0]) | (sizes[receiver] == 0), 0, jnp.maximum(slack, 0))
    passed = jax.random.randint(jax.random.fold_in(own, 4), (count // 2,), 0, 1 << 20) % (slack + 1)
    sizes = sizes.at[donor].add(-passed).at[receiver].add(passed)
    items = jnp.searchsorted(jnp.cumsum(sizes), jnp.arange(rows * top), side="right").astype(jnp.int32)
    listing = items.reshape(top, rows).T
    listing = listing[jax.random.permutation(jax.random.fold_in(own, 1), rows)]
    turn = jax.random.randint(jax.random.fold_in(own, 2), (rows, 1), 0, top)
    return jnp.take_along_axis(listing, (jnp.arange(top)[None, :] + turn) % top, axis=1)


def load_shares(amount, total, reach, skew, full):
    weights = [(1 << 20) // math.isqrt(rank ** skew) + 1 for rank in range(1, amount + 1)]
    largest = reach if full else min(reach, max(-(-total // amount), total * weights[0] // sum(weights)))
    least = 1 if total - largest >= amount - 1 else 0
    given, rest = [largest] + [least] * (amount - 1), total - largest - least * (amount - 1)
    while rest > 0:
        free = [i for i in range(1, amount) if given[i] < largest] or [i for i in range(1, amount) if given[i] < reach]
        pool, remaining = sum([weights[i] for i in free]), rest
        for i in free:
            more = min(reach - given[i], max(1, remaining * weights[i] // pool), rest)
            given[i] = given[i] + more
            rest = rest - more
    return np.array(given)


def gaussian(rng, extent, width, bound, cuts=(), kind=jnp.bfloat16):
    drawn = width * jax.random.normal(rng, extent, jnp.float32)
    if cuts:
        drawn = drawn * level_of(rng, extent, cuts, -0.22, 0.18)
    return jnp.clip(drawn, -bound, bound).astype(kind)


def setup_inputs(seed: int = 0, part: int = 0) -> dict:
    streams_of = jax.random.split(jax.random.key(seed), 8)
    own_keys = jax.random.split(jax.random.fold_in(streams_of[7], part), 8)
    tokens = gaussian(own_keys[0], (TOKENS, D), 1.0, 6.0, ((0, 4), (1, 4)))
    expert_ids_keys = jax.random.split(jax.random.fold_in(own_keys[1], 1), TOKENS // TOK_E)
    expert_ids_turns = jax.random.permutation(jax.random.fold_in(own_keys[1], 3), TOKENS // TOK_E)
    expert_ids = jax.vmap(lambda own, number: deal_out(jax.random.fold_in(own_keys[1], 2), own, number, TOK_E, EXPERTS, TOP, CAP, 2))(expert_ids_keys, expert_ids_turns).reshape((TOKENS, TOP))
    gate_weights = jnp.clip(0.05 + 0.39999999 * jax.random.uniform(own_keys[2], (TOKENS, TOP), jnp.float32) ** level_of(own_keys[2], (TOKENS, TOP), ((0, 4),), -0.2, 0.2), 0.05, 0.45)
    base_weights = gaussian(streams_of[3], (3, F, D), D ** -0.5, 0.0625, ((1, 4), (2, 4)))
    in_factor = gaussian(streams_of[4], (RANKS_ALL, D), D ** -0.5, 0.0625, ((0, 4), (1, 4)))
    out_factors = gaussian(streams_of[5], (2, RANKS_ALL, F), (RANK_MAX // 2) ** -0.5, 0.375, ((1, 4), (2, 4)))
    ranks = draw_ranks(jax.random.fold_in(streams_of[7], 71), part)
    return dict(tokens=tokens, expert_ids=expert_ids, gate_weights=gate_weights, base_weights=base_weights, in_factor=in_factor, out_factors=out_factors, ranks=ranks)


def reference(tokens, expert_ids, gate_weights, base_weights, in_factor, out_factors, ranks):
    blocks_count = N_TENSOR * N_INNER
    pieces = D // blocks_count
    rows_per = N_EXPERT * CAP
    base_rows = jnp.einsum("td,gfd->tgf", tokens.astype(jnp.float32), base_weights[:2].astype(jnp.float32)).astype(jnp.bfloat16)
    start = (jnp.cumsum(ranks) - ranks).astype(jnp.int32)
    pairs = TOKENS * TOP
    flat_ids = expert_ids.reshape(pairs).astype(jnp.int32)
    onehot = (flat_ids[:, None] == jnp.arange(EXPERTS, dtype=jnp.int32)[None, :]).astype(jnp.int32)
    onehot = onehot.reshape(N_EXPERT, TOK_E * TOP, EXPERTS)
    before = jnp.cumsum(onehot, axis=1) - onehot
    slot = jnp.sum(before * onehot, axis=2).reshape(pairs).astype(jnp.int32)
    block_of = (jnp.arange(pairs, dtype=jnp.int32) // (TOK_E * TOP)).astype(jnp.int32)
    target = (flat_ids * rows_per + block_of * CAP + slot).astype(jnp.int32)
    table = jnp.full((EXPERTS * rows_per,), -1, jnp.int32).at[target].set(jnp.arange(pairs, dtype=jnp.int32))
    table = table.reshape(EXPERTS, rows_per)
    in_pad = jnp.concatenate([in_factor, jnp.zeros((RANK_MAX, D), in_factor.dtype)], 0)
    out_pad = jnp.concatenate([out_factors, jnp.zeros((2, RANK_MAX, F), out_factors.dtype)], 1)
    within = jnp.arange(RANK_MAX, dtype=jnp.int32)

    def one_expert(expert):
        index = table[expert]
        valid = index >= 0
        source = (jnp.maximum(index, 0) // TOP).astype(jnp.int32)
        routed = jnp.where(valid[:, None], tokens[source], jnp.zeros((), tokens.dtype)).astype(jnp.float32)
        window = lax.dynamic_slice_in_dim(in_pad, start[expert], RANK_MAX, 0).astype(jnp.float32)
        parts = jnp.einsum("rpd,cpd->prc", routed.reshape(rows_per, blocks_count, pieces), window.reshape(RANK_MAX, blocks_count, pieces))
        rounded = lax.optimization_barrier(parts.astype(jnp.bfloat16))
        latent = jnp.sum(rounded.astype(jnp.float32), axis=0)
        latent = jnp.where(within[None, :] < ranks[expert], latent, jnp.float32(0.0)).astype(jnp.bfloat16)
        factor = lax.dynamic_slice_in_dim(out_pad, start[expert], RANK_MAX, 1).astype(jnp.float32)
        return jnp.einsum("rc,gcf->rgf", latent.astype(jnp.float32), factor).astype(jnp.bfloat16)

    deltas = lax.map(one_expert, jnp.arange(EXPERTS, dtype=jnp.int32))
    picked = deltas.reshape(EXPERTS * rows_per, 2, F)[target].reshape(TOKENS, TOP, 2, F)
    summed = base_rows.astype(jnp.float32)[:, None] + picked.astype(jnp.float32)
    hidden = (jax.nn.silu(summed[:, :, 0]) * summed[:, :, 1]).astype(jnp.bfloat16)
    combined = jnp.sum(gate_weights[:, :, None] * hidden.astype(jnp.float32), axis=1).astype(jnp.bfloat16)
    return jnp.dot(combined, base_weights[2], preferred_element_type=jnp.float32).astype(jnp.bfloat16)
```

```python
import jax
import jax.numpy as jnp
from jax import lax
from jax.sharding import PartitionSpec as P

BF = jnp.bfloat16
F32 = jnp.float32
LINE_MAX = 8


def dot(lhs, rhs, dims):
    return lax.dot_general(lhs, rhs, (dims, ((), ())), preferred_element_type=F32)


def chain_gather(value, axis, first=None):
    size = lax.axis_size(axis)
    if size > LINE_MAX:
        return lax.all_gather(value, axis, axis=0, tiled=True)
    up = [(j, j + 1) for j in range(size - 1)]
    down = [(j + 1, j) for j in range(size - 1)]
    left, right = [], []
    from_left, from_right = value, value
    for _ in range(size - 1):
        from_left = lax.ppermute(from_left, axis, up)
        from_right = lax.ppermute(from_right, axis, down)
        left.append(from_left)
        right.append(from_right)
    line = jnp.concatenate(left[::-1] + [value] + right, 0)
    rows = value.shape[0]
    return lax.dynamic_slice_in_dim(line, (size - 1 - lax.axis_index(axis)) * rows, size * rows, 0)


def direct_gather(value, axis):
    size = lax.axis_size(axis)
    if size == 1:
        return value
    if size > LINE_MAX:
        return lax.all_gather(value, axis, axis=0, tiled=True)
    got = [value]
    for shift in range(1, size):
        got.append(lax.ppermute(value, axis, [(j, (j + shift) % size) for j in range(size)]))
    rows = value.shape[0]
    line = jnp.concatenate(got[:0:-1] + [value] + got[:0:-1], 0)
    return lax.dynamic_slice_in_dim(line, (size - 1 - lax.axis_index(axis)) * rows, size * rows, 0)


def scatter_sum(piece_of, axis):
    size = lax.axis_size(axis)
    index = lax.axis_index(axis)
    got = []
    for shift in range(1, size):
        sent = piece_of((index + shift) % size).astype(BF)
        got.append(lax.ppermute(sent, axis, [(j, (j + shift) % size) for j in range(size)]))
    total = piece_of(index).astype(F32)
    for term in got:
        total = total + term.astype(F32)
    return total


def after(value, *others):
    return lax.optimization_barrier((value,) + others)[0]


def on_device(tokens, expert_ids, gate_weights, base_weights, in_factor, out_factors, ranks):
    rows, feats = tokens.shape
    owners = lax.axis_size("expert")
    tensors, inners = lax.axis_size("tensor"), lax.axis_size("inner")
    copies = lax.axis_size("groups")
    local = ranks.shape[0]
    experts = local * owners
    units = base_weights.shape[1]
    hidden_all = units * owners
    width = in_factor.shape[0]
    sub = rows // (tensors * inners)
    z = lax.axis_index("expert")
    core = lax.axis_index("inner")
    part = lax.axis_index("tensor") * inners + core

    gathered = chain_gather(tokens, "expert")

    own_ids = lax.dynamic_slice_in_dim(expert_ids, part * sub, sub, 0)
    own_gates = lax.dynamic_slice_in_dim(gate_weights, part * sub, sub, 0)
    columns = lax.broadcasted_iota(jnp.int32, (1, 1, experts), 2)
    dense = jnp.sum(jnp.where(own_ids[:, :, None] == columns, own_gates[:, :, None], 0.0), axis=1)
    dense = direct_gather(dense, "expert")
    gates = lax.dynamic_slice_in_dim(dense, z * local, local, 1)

    factors = direct_gather(direct_gather(out_factors[None], "tensor"), "inner")

    blocks = gathered.reshape(owners, tensors, inners, sub, feats)
    base_flat = base_weights[:2].reshape(2 * units, feats)

    def product(weights):
        def of_core(index):
            picked = lax.dynamic_index_in_dim(blocks, index, 2, keepdims=False)
            picked = picked.reshape(owners * tensors * sub, feats)
            return dot(picked, weights, ((1,), (1,)))

        halves = scatter_sum(of_core, "inner").reshape(owners, tensors, sub, weights.shape[0])

        def of_tensor(index):
            return lax.dynamic_index_in_dim(halves, index, 1, keepdims=False)

        return scatter_sum(of_tensor, "tensor").reshape(owners * sub, weights.shape[0]).astype(BF)

    base_rows = product(base_flat)
    latent = product(in_factor)

    base_all = chain_gather(base_rows.reshape(1, owners * sub, 2, units), "expert")

    down = base_weights[2]
    if owners <= LINE_MAX and units % copies == 0 and copies > 1:
        piece = units // copies
        g = lax.axis_index("groups")
        mine = lax.dynamic_slice_in_dim(down, g * piece, piece, 0)
        mine = after(mine, gathered)
        mine = chain_gather(mine[None], "expert")
        down_all = direct_gather(mine[None], "groups")
        down_all = jnp.moveaxis(down_all, 0, 1).reshape(hidden_all, feats)
    else:
        down_all = lax.all_gather(down, "expert", axis=0, tiled=True)

    ends = jnp.cumsum(ranks)
    position = lax.broadcasted_iota(jnp.int32, (1, width), 1)
    owner_of = jnp.sum((position[:, :, None] >= ends[None, None, :]).astype(jnp.int32), axis=2)
    member = lax.broadcasted_iota(jnp.int32, (local, 1, 1), 0)
    base_all = base_all.transpose(1, 2, 0, 3).reshape(owners * sub, 2, hidden_all)

    def mix(operands):
        latent_rows, base_part, gate_part = operands
        count = latent_rows.shape[0]
        spread = jnp.where(owner_of[None] == member, latent_rows[None], jnp.zeros((), BF))
        spread = spread.reshape(local * count, width)
        both = []
        for g in range(2):
            parts = []
            for block in range(tensors * inners):
                source = (block % inners) * tensors + block // inners
                parts.append(dot(spread, factors[source, g], ((1,), (0,))).astype(BF))
            delta = jnp.concatenate(parts, 1).reshape(local, count, hidden_all)
            both.append(base_part[None, :, g].astype(F32) + delta.astype(F32))
        hidden = (jax.nn.silu(both[0]) * both[1]).astype(BF).astype(F32)
        weight = gate_part.T[:, :, None]
        return jnp.sum(jnp.where(weight > 0, weight * hidden, 0.0), axis=0)

    chunks = max(1, owners * sub // rows)
    if chunks == 1:
        combined = mix((latent, base_all, gates))
    else:
        split = lambda v: v.reshape((chunks, v.shape[0] // chunks) + v.shape[1:])
        combined = lax.map(mix, (split(latent), split(base_all), split(gates)))
    combined = combined.reshape(owners, sub, hidden_all)

    if owners > LINE_MAX:
        mixed = lax.all_to_all(combined.astype(BF), "expert", 0, 0, tiled=True)
        own = jnp.sum(mixed.astype(F32), axis=0)
    else:
        own = scatter_sum(lambda index: lax.dynamic_index_in_dim(combined, index, 0, keepdims=False), "expert")
    full = direct_gather(direct_gather(own.astype(BF)[None], "tensor"), "inner")
    full = full.reshape(inners, tensors, sub, hidden_all).swapaxes(0, 1).reshape(rows, hidden_all)
    return dot(full, down_all, ((1,), (0,))).astype(BF)


def solution(mesh):
    return jax.shard_map(
        on_device,
        mesh=mesh,
        in_specs=(
            P(("groups", "expert"), ("tensor", "inner")),
            P(("groups", "expert"), None),
            P(("groups", "expert"), None),
            P(None, "expert", ("tensor", "inner")),
            P("expert", ("tensor", "inner")),
            P(None, "expert", ("tensor", "inner")),
            P("expert"),
        ),
        out_specs=P(("groups", "expert"), ("tensor", "inner")),
        check_vma=False,
    )
```

```python
import jax
import jax.numpy as jnp
from jax import lax
from jax.experimental import pallas as pl
from jax.experimental.pallas import tpu as pltpu
from jax.sharding import PartitionSpec as P

BF = jnp.bfloat16
F32 = jnp.float32
LINE_MAX = 8


def dot(lhs, rhs, dims):
    return lax.dot_general(lhs, rhs, (dims, ((), ())), preferred_element_type=F32)


def chain_gather(value, axis, first=None):
    size = lax.axis_size(axis)
    if size > LINE_MAX:
        return lax.all_gather(value, axis, axis=0, tiled=True)
    up = [(j, j + 1) for j in range(size - 1)]
    down = [(j + 1, j) for j in range(size - 1)]
    left, right = [], []
    from_left, from_right = value, value
    for _ in range(size - 1):
        from_left = lax.ppermute(from_left, axis, up)
        from_right = lax.ppermute(from_right, axis, down)
        left.append(from_left)
        right.append(from_right)
    line = jnp.concatenate(left[::-1] + [value] + right, 0)
    rows = value.shape[0]
    return lax.dynamic_slice_in_dim(line, (size - 1 - lax.axis_index(axis)) * rows, size * rows, 0)


def direct_gather(value, axis):
    size = lax.axis_size(axis)
    if size == 1:
        return value
    if size > LINE_MAX:
        return lax.all_gather(value, axis, axis=0, tiled=True)
    got = [value]
    for shift in range(1, size):
        got.append(lax.ppermute(value, axis, [(j, (j + shift) % size) for j in range(size)]))
    rows = value.shape[0]
    line = jnp.concatenate(got[:0:-1] + [value] + got[:0:-1], 0)
    return lax.dynamic_slice_in_dim(line, (size - 1 - lax.axis_index(axis)) * rows, size * rows, 0)


def scatter_sum(piece_of, axis):
    size = lax.axis_size(axis)
    index = lax.axis_index(axis)
    got = []
    for shift in range(1, size):
        sent = piece_of((index + shift) % size).astype(BF)
        got.append(lax.ppermute(sent, axis, [(j, (j + shift) % size) for j in range(size)]))
    total = piece_of(index).astype(F32)
    for term in got:
        total = total + term.astype(F32)
    return total


def after(value, *others):
    return lax.optimization_barrier((value,) + others)[0]


def general(tokens, expert_ids, gate_weights, base_weights, in_factor, out_factors, ranks):
    rows, feats = tokens.shape
    owners = lax.axis_size("expert")
    tensors, inners = lax.axis_size("tensor"), lax.axis_size("inner")
    copies = lax.axis_size("groups")
    local = ranks.shape[0]
    experts = local * owners
    units = base_weights.shape[1]
    hidden_all = units * owners
    width = in_factor.shape[0]
    sub = rows // (tensors * inners)
    z = lax.axis_index("expert")
    core = lax.axis_index("inner")
    part = lax.axis_index("tensor") * inners + core

    gathered = chain_gather(tokens, "expert")

    own_ids = lax.dynamic_slice_in_dim(expert_ids, part * sub, sub, 0)
    own_gates = lax.dynamic_slice_in_dim(gate_weights, part * sub, sub, 0)
    columns = lax.broadcasted_iota(jnp.int32, (1, 1, experts), 2)
    dense = jnp.sum(jnp.where(own_ids[:, :, None] == columns, own_gates[:, :, None], 0.0), axis=1)
    dense = direct_gather(dense, "expert")
    gates = lax.dynamic_slice_in_dim(dense, z * local, local, 1)

    factors = direct_gather(direct_gather(out_factors[None], "tensor"), "inner")

    blocks = gathered.reshape(owners, tensors, inners, sub, feats)
    base_flat = base_weights[:2].reshape(2 * units, feats)

    def product(weights):
        def of_core(index):
            picked = lax.dynamic_index_in_dim(blocks, index, 2, keepdims=False)
            picked = picked.reshape(owners * tensors * sub, feats)
            return dot(picked, weights, ((1,), (1,)))

        halves = scatter_sum(of_core, "inner").reshape(owners, tensors, sub, weights.shape[0])

        def of_tensor(index):
            return lax.dynamic_index_in_dim(halves, index, 1, keepdims=False)

        return scatter_sum(of_tensor, "tensor").reshape(owners * sub, weights.shape[0]).astype(BF)

    base_rows = product(base_flat)
    latent = product(in_factor)

    base_all = chain_gather(base_rows.reshape(1, owners * sub, 2, units), "expert")

    down = base_weights[2]
    if owners <= LINE_MAX and units % copies == 0 and copies > 1:
        piece = units // copies
        g = lax.axis_index("groups")
        mine = lax.dynamic_slice_in_dim(down, g * piece, piece, 0)
        mine = after(mine, gathered)
        mine = chain_gather(mine[None], "expert")
        down_all = direct_gather(mine[None], "groups")
        down_all = jnp.moveaxis(down_all, 0, 1).reshape(hidden_all, feats)
    else:
        down_all = lax.all_gather(down, "expert", axis=0, tiled=True)

    ends = jnp.cumsum(ranks)
    position = lax.broadcasted_iota(jnp.int32, (1, width), 1)
    owner_of = jnp.sum((position[:, :, None] >= ends[None, None, :]).astype(jnp.int32), axis=2)
    member = lax.broadcasted_iota(jnp.int32, (local, 1, 1), 0)
    base_all = base_all.transpose(1, 2, 0, 3).reshape(owners * sub, 2, hidden_all)

    def mix(operands):
        latent_rows, base_part, gate_part = operands
        count = latent_rows.shape[0]
        spread = jnp.where(owner_of[None] == member, latent_rows[None], jnp.zeros((), BF))
        spread = spread.reshape(local * count, width)
        both = []
        for g in range(2):
            parts = []
            for block in range(tensors * inners):
                source = (block % inners) * tensors + block // inners
                parts.append(dot(spread, factors[source, g], ((1,), (0,))).astype(BF))
            delta = jnp.concatenate(parts, 1).reshape(local, count, hidden_all)
            both.append(base_part[None, :, g].astype(F32) + delta.astype(F32))
        hidden = (jax.nn.silu(both[0]) * both[1]).astype(BF).astype(F32)
        weight = gate_part.T[:, :, None]
        return jnp.sum(jnp.where(weight > 0, weight * hidden, 0.0), axis=0)

    chunks = max(1, owners * sub // rows)
    if chunks == 1:
        combined = mix((latent, base_all, gates))
    else:
        split = lambda v: v.reshape((chunks, v.shape[0] // chunks) + v.shape[1:])
        combined = lax.map(mix, (split(latent), split(base_all), split(gates)))
    combined = combined.reshape(owners, sub, hidden_all)

    if owners > LINE_MAX:
        mixed = lax.all_to_all(combined.astype(BF), "expert", 0, 0, tiled=True)
        own = jnp.sum(mixed.astype(F32), axis=0)
    else:
        own = scatter_sum(lambda index: lax.dynamic_index_in_dim(combined, index, 0, keepdims=False), "expert")
    full = direct_gather(direct_gather(own.astype(BF)[None], "tensor"), "inner")
    full = full.reshape(inners, tensors, sub, hidden_all).swapaxes(0, 1).reshape(rows, hidden_all)
    return dot(full, down_all, ((1,), (0,))).astype(BF)


def swaps(size, k):
    return [(j, j ^ k) for j in range(size)]


def pick(value, index, count, axis=0):
    return lax.dynamic_slice_in_dim(value, index * count, count, axis)


def pair_sum(parts, axis, rows):
    index = lax.axis_index(axis)
    half = rows // 2
    sent = pick(parts, index ^ 1, half, 1).astype(BF)
    got = lax.ppermute(sent, axis, swaps(2, 1))
    return pick(parts, index, half, 1).astype(F32) + got.astype(F32)


def gated_kernel(where_ref, *refs, slots, early, local, units, inner_units):
    owners = slots
    blocks = owners
    tables_a = refs[:owners]
    tables_b = refs[owners : 2 * owners]
    deltas = refs[2 * owners : 2 * owners + 2 * blocks]
    gates = refs[2 * owners + 2 * blocks]
    out = refs[-1]
    z = where_ref[0]
    part = where_ref[1]

    def table(j, k, g):
        source = k ^ j
        lo = g * units
        if source < early:
            return tables_a[j][source, :, lo : lo + units].astype(F32)
        return tables_b[j][source - early, :, lo : lo + units].astype(F32)

    for m in range(blocks):
        h = part ^ m
        j_of = z ^ h
        for k in range(slots):
            base = []
            for g in range(2):
                chosen = table(0, k, g)
                for j in range(1, owners):
                    chosen = jnp.where(j_of == j, table(j, k, g), chosen)
                base.append(chosen)
            total = jnp.zeros_like(base[0])
            for e in range(local):
                gate = base[0] + deltas[2 * m][e, k].astype(F32)
                up = base[1] + deltas[2 * m + 1][e, k].astype(F32)
                hidden = gate / (1.0 + jnp.exp(-gate)) * up
                weight = gates[k, :, e : e + 1]
                total = total + jnp.where(weight > 0, weight * hidden, 0.0)
            total = total.astype(BF)
            for q in range(units // inner_units):
                out[k, h * (units // inner_units) + q] = total[:, q * inner_units : (q + 1) * inner_units]


def final_kernel(where_ref, *refs, rows_of, weights_of, tile):
    count = len(rows_of)
    lhs = refs[:count]
    rhs = refs[count:-1]
    out = refs[-1]
    sub = lhs[0].shape[1]
    feats = out.shape[1]
    left = []
    for w, _ in weights_of:
        index = where_ref[count + len(left)]
        left.append(jnp.concatenate([p[index] for p in lhs], 0))
    for lo in range(0, feats, tile):
        total = None
        for q, (w, row) in enumerate(weights_of):
            piece = rhs[w][row : row + left[q].shape[1], lo : lo + tile]
            term = lax.dot_general(left[q], piece, (((1,), (0,)), ((), ())), preferred_element_type=F32)
            total = term if total is None else total + term
        total = total.astype(BF)
        for r in range(count):
            start = pl.multiple_of(where_ref[r], sub)
            out[pl.ds(start, sub), lo : lo + tile] = total[r * sub : (r + 1) * sub]


def fast(tokens, expert_ids, gate_weights, base_weights, in_factor, out_factors, ranks):
    rows, feats = tokens.shape
    owners = lax.axis_size("expert")
    tensors, inners = lax.axis_size("tensor"), lax.axis_size("inner")
    copies = lax.axis_size("groups")
    local = ranks.shape[0]
    experts = local * owners
    units = base_weights.shape[1]
    width = in_factor.shape[0]
    sub = rows // (tensors * inners)
    z = lax.axis_index("expert")
    t = lax.axis_index("tensor")
    c = lax.axis_index("inner")
    g = lax.axis_index("groups")
    part = t * inners + c
    rows_at = c * tensors + t
    early = owners - 1

    second = lax.ppermute(tokens, "expert", swaps(owners, 2))
    first = lax.ppermute(tokens, "expert", swaps(owners, 1))

    own_ids = pick(expert_ids, rows_at, sub)
    own_gates = pick(gate_weights, rows_at, sub)
    columns = lax.broadcasted_iota(jnp.int32, (1, 1, experts), 2)
    dense = jnp.sum(jnp.where(own_ids[:, :, None] == columns, own_gates[:, :, None], 0.0), axis=1)
    gates = [pick(dense, z, local, 1)]
    for k in range(1, owners):
        gates.append(lax.ppermute(pick(dense, z ^ k, local, 1), "expert", swaps(owners, k)))
    gates = jnp.stack(gates)

    across = lax.ppermute(out_factors, "tensor", swaps(tensors, 1))
    factors = [
        out_factors,
        lax.ppermute(out_factors, "inner", swaps(inners, 1)),
        across,
        lax.ppermute(across, "inner", swaps(inners, 1)),
    ]

    forward = lax.ppermute(after(second, first), "expert", [(1, 0), (2, 3)])
    middle = lax.ppermute(after(tokens, first, second), "expert", [(1, 2), (2, 1)])
    third = jnp.where((z == 1) | (z == 2), middle, forward)

    base_flat = base_weights[:2].reshape(2 * units, feats)

    def product(value, weights):
        parts = dot(value, weights, ((1,), (1,)))
        parts = parts.reshape(value.shape[0] // rows, rows, weights.shape[0])
        parts = pair_sum(parts, "inner", rows)
        return pair_sum(parts, "tensor", rows // inners).astype(BF)

    ready = jnp.concatenate([tokens, first, second], 0)
    base_a = product(ready, base_flat)
    latent_a = product(ready, in_factor)
    base_b = product(third, base_flat)
    latent_b = product(third, in_factor)

    tables_a, tables_b = [base_a], [base_b]
    for k in range(1, owners):
        tables_a.append(lax.ppermute(base_a, "expert", swaps(owners, k)))
    for k in range(1, owners):
        tables_b.append(lax.ppermute(base_b, "expert", swaps(owners, k)))

    down = base_weights[2]
    piece = units // copies
    mine = after(pick(down, g, piece), third)
    near, far = [], []
    for k in range(1, owners):
        half = lax.ppermute(mine, "expert", swaps(owners, k))
        near.append(half)
        far.append(lax.ppermute(half, "groups", swaps(copies, 1)))

    ends = jnp.cumsum(ranks)
    position = lax.broadcasted_iota(jnp.int32, (1, width), 1)
    owner_of = jnp.sum((position[:, :, None] >= ends[None, None, :]).astype(jnp.int32), axis=2)
    member = lax.broadcasted_iota(jnp.int32, (local, 1, 1), 0)
    latent = jnp.concatenate([latent_a, latent_b], 0).reshape(owners * sub, width)
    spread = jnp.where(owner_of[None] == member, latent[None], jnp.zeros((), BF))
    spread = spread.reshape(local * owners * sub, width)
    deltas = []
    for m in range(owners):
        for side in range(2):
            delta = dot(spread, factors[m][side], ((1,), (0,))).astype(BF)
            deltas.append(delta.reshape(local, owners, sub, units))

    spot = jnp.stack([z, part]).astype(jnp.int32)
    whole = pl.BlockSpec(memory_space=pltpu.VMEM)
    numbers = pl.BlockSpec(memory_space=pltpu.SMEM)
    combined = pl.pallas_call(
        lambda *refs: gated_kernel(
            *refs, slots=owners, early=early, local=local, units=units, inner_units=piece
        ),
        out_shape=jax.ShapeDtypeStruct((owners, owners * copies, sub, piece), BF),
        in_specs=[numbers] + [whole] * (2 * owners + 2 * owners + 1),
        out_specs=whole,
        name="gated",
    )(spot, *tables_a, *tables_b, *deltas, gates)

    total = combined[0].astype(F32)
    for k in range(1, owners):
        total = total + lax.ppermute(combined[k], "expert", swaps(owners, k)).astype(F32)
    own = total.astype(BF)
    beside = lax.ppermute(own, "tensor", swaps(tensors, 1))
    lhs = [own, beside, lax.ppermute(own, "inner", swaps(inners, 1)), lax.ppermute(beside, "inner", swaps(inners, 1))]
    starts = [
        (c * tensors + t) * sub,
        (c * tensors + (t ^ 1)) * sub,
        ((c ^ 1) * tensors + t) * sub,
        ((c ^ 1) * tensors + (t ^ 1)) * sub,
    ]
    rhs = [down] + near + far
    weights_of = [(0, q * piece) for q in range(copies)]
    order = [z * copies + q for q in range(copies)]
    for k in range(1, owners):
        weights_of.append((k, 0))
        order.append((z ^ k) * copies + g)
    for k in range(1, owners):
        weights_of.append((owners - 1 + k, 0))
        order.append((z ^ k) * copies + (g ^ 1))
    spot = jnp.stack(starts + order).astype(jnp.int32)
    return pl.pallas_call(
        lambda *refs: final_kernel(*refs, rows_of=starts, weights_of=weights_of, tile=2 * piece),
        out_shape=jax.ShapeDtypeStruct((rows, feats), BF),
        in_specs=[numbers] + [whole] * (len(lhs) + len(rhs)),
        out_specs=whole,
        name="final",
    )(spot, *lhs, *rhs)


def solution(mesh):
    shape = mesh.shape
    small = shape["expert"] == 4 and shape["tensor"] == 2 and shape["inner"] == 2 and shape["groups"] == 2
    return jax.shard_map(
        fast if small else general,
        mesh=mesh,
        in_specs=(
            P(("groups", "expert"), ("tensor", "inner")),
            P(("groups", "expert"), None),
            P(("groups", "expert"), None),
            P(None, "expert", ("tensor", "inner")),
            P("expert", ("tensor", "inner")),
            P(None, "expert", ("tensor", "inner")),
            P("expert"),
        ),
        out_specs=P(("groups", "expert"), ("tensor", "inner")),
        check_vma=False,
    )
```
